32 devices in a mesh: gx: 8 (over z, x), gy: 4 (over y, core).
Axes of the slice: x: 2, y: 2, z: 4, core: 2. Of those that a mesh axis runs over, the one named last changes fastest.
Arguments:
- velocity: float32 [3, 16, 1024, 512], P(None, None, 'gx', 'gy'), may hold values from -6 to 6
- inv_x: float32 [1024, 128], P('gx'), as said below
- inv_y: float32 [512, 128], P('gy'), as said below
- spike_x: float32 [1024, 2], P('gx'), as said below
- spike_y: float32 [512, 2], P('gy'), as said below
- marker_force: bfloat16 [3, 65536], P(None, ('gx', 'gy')), may hold values from -6 to 6
- marker_kernel: bfloat16 [65536, 128], P(('gx', 'gy')), may hold values from 0 to 1
- marker_owner: int32 [65536, 1], P(('gx', 'gy')), may hold values from 0 to 7; in each aligned block of 2048 rows (0 to 2047, 2048 to 4095, ...) at most 512 rows name the same one
- marker_row: int32 [65536], P(('gx', 'gy')), may hold values from 0 to 2047
Outputs:
- section_velocity: float32 [3, 16, 1024, 512], P(None, None, 'gx', 'gy')
The draws below stay inside these ranges and needn't reach their ends.
Inputs may be any that keep to these rules, and one draw needn't show every extreme that they name: `marker_owner`: among the 2048 marker slots of one device, no owner is named more than 512 times, a bound that some block reaches; every owner is named somewhere. `inv_x`: one block for each streamwise block of cells. `inv_y`: one block for each spanwise block of cells. `spike_x`: two columns for each streamwise block of cells. `spike_y`: two columns for each spanwise block of cells.
All inputs are finite; a program needn't handle non-finite values.
Results may differ from the reference program's by a relative error of at most 0.00046.
Values may be sent and summed in bfloat16 or wider, within the bound.
No kernel may reach another device: no remote copies, remote signals or barrier semaphores. Data moves between devices by JAX's collectives and lax.ppermute only.
A program may use at most 128 MiB of HBM per device.

```python
import math
import jax
import jax.numpy as jnp
import numpy as np
from jax import lax

NZ = 16
CX = 128
CY = 128
M_DEV = 2048
NX = 1024
NY = 512
MARKERS = 65536
CAP = 512
N_GX = 8
N_GY = 4


def block_draw(key, rows, width):
    first, second = jax.random.split(key)
    local = lax.broadcasted_iota(jnp.int32, (rows, width), 0) % width
    column = lax.broadcasted_iota(jnp.int32, (rows, width), 1)
    spread = 0.5 / width ** 0.5
    off = jax.random.normal(first, (rows, width), jnp.float32) * spread
    main = jax.random.uniform(second, (rows, width), jnp.float32, 0.8, 1.2)
    return jnp.where(local == column, main, off)


def spike_draw(key, rows, width):
    first, second, third = jax.random.split(key, 3)
    local = lax.broadcasted_iota(jnp.int32, (rows, 2), 0) % width
    column = lax.broadcasted_iota(jnp.int32, (rows, 2), 1)
    body_part = jax.random.normal(first, (rows, 2), jnp.float32) * 0.4
    keep = jax.random.uniform(second, (rows, 2), jnp.float32, 0.92, 0.99)
    cross = jax.random.uniform(third, (rows, 2), jnp.float32, -0.03, 0.03)
    tail = jnp.where(local - (width - 2) == column, keep, cross)
    return jnp.where(local >= width - 2, tail, body_part)


def draw_inv_x(key, part):
    return block_draw(jax.random.fold_in(key, 11), NX, CX)


def draw_inv_y(key, part):
    return block_draw(jax.random.fold_in(key, 12), NY, CY)


def draw_spike_x(key, part):
    return spike_draw(jax.random.fold_in(key, 13), NX, CX)


def draw_spike_y(key, part):
    return spike_draw(jax.random.fold_in(key, 14), NY, CY)


def plant(entries, stream_key, least, largest):
    spot = [jax.random.randint(jax.random.fold_in(stream_key, axis), (), 0, length) for axis, length in enumerate(entries.shape)]
    longest = entries.shape.index(max(entries.shape))
    next_to = spot[:longest] + [(spot[longest] + 1) % entries.shape[longest]] + spot[longest + 1:]
    return entries.at[tuple(spot)].set(least).at[tuple(next_to)].set(largest)


def shard_levels(own_key, extent, pieces, smallest, top_value):
    def one(position, shards_of):
        draws = jax.random.uniform(jax.random.fold_in(jax.random.fold_in(own_key, 6), position), (shards_of,), jnp.float32, smallest / len(pieces), top_value / len(pieces))
        return jnp.repeat(jnp.exp(draws), extent[position] // shards_of).reshape((-1,) + (1,) * (len(extent) - position - 1))

    gain = one(*pieces[0])
    for cut in pieces[1:]:
        gain = gain * one(*cut)
    return gain


def deal_out(own_key, own, number, rows, count, top, bound, skew):
    ranking = jax.random.permutation(own_key, count)
    heavy_load, common = shares(count, rows * top, bound, skew, True), shares(count, rows * top, bound, skew, False)
    places = jnp.arange(count)

    def named(lengths, turn):
        used = int((lengths > 0).sum())
        fixed = max(1, used // 4)
        shifted = fixed + (places - fixed + turn * (used - fixed)) % max(1, count - fixed)
        return jnp.zeros((count,), jnp.int32).at[ranking[jnp.where(places < fixed, places, shifted)]].set(jnp.asarray(lengths, jnp.int32))

    lengths = jnp.where(number % 4 == 0, named(heavy_load, number // 4), named(common, number - number // 4 - 1))
    mixed = jax.random.permutation(jax.random.fold_in(own, 3), count)
    source_of, taker = mixed[0:count // 2 * 2:2], mixed[1:count // 2 * 2:2]
    room = jnp.minimum(lengths[source_of] - 1, bound - lengths[taker]) // 2
    room = jnp.where((source_of == ranking[0]) | (taker == ranking[0]) | (lengths[taker] == 0), 0, jnp.maximum(room, 0))
    shifted = jax.random.randint(jax.random.fold_in(own, 4), (count // 2,), 0, 1 << 20) % (room + 1)
    lengths = lengths.at[source_of].add(-shifted).at[taker].add(shifted)
    items = jnp.searchsorted(jnp.cumsum(lengths), jnp.arange(rows * top), side="right").astype(jnp.int32)
    listing = items.reshape(top, rows).T
    listing = listing[jax.random.permutation(jax.random.fold_in(own, 1), rows)]
    turn = jax.random.randint(jax.random.fold_in(own, 2), (rows, 1), 0, top)
    return jnp.take_along_axis(listing, (jnp.arange(top)[None, :] + turn) % top, axis=1)


def shares(amount, total, reach, lean, full):
    loads = [(1 << 20) // math.isqrt(rank ** lean) + 1 for rank in range(1, amount + 1)]
    largest = reach if full else min(reach, max(-(-total // amount), total * loads[0] // sum(loads)))
    least = 1 if total - largest >= amount - 1 else 0
    counts, rest = [largest] + [least] * (amount - 1), total - largest - least * (amount - 1)
    while rest > 0:
        candidates = [i for i in range(1, amount) if counts[i] < largest] or [i for i in range(1, amount) if counts[i] < reach]
        whole, budget = sum([loads[i] for i in candidates]), rest
        for i in candidates:
            extra = min(reach - counts[i], max(1, budget * loads[i] // whole), rest)
            counts[i] = counts[i] + extra
            rest = rest - extra
    return np.array(counts)


def noise(stream_key, extent, deviation, most, cuts=(), held_as=jnp.bfloat16):
    level = shard_levels(stream_key, extent, cuts, -0.22, 0.18) if cuts else 1.0
    values = jax.random.normal(stream_key, extent, jnp.float32) * deviation * level
    return jnp.minimum(jnp.maximum(values, -most), most).astype(held_as)


def setup_inputs(seed: int = 0) -> dict:
    arg_keys = jax.random.split(jax.random.key(seed), 10)
    velocity = noise(arg_keys[0], (3, NZ, NX, NY), 1.0, 6.0, ((2, 8), (3, 4)), jnp.float32)
    inv_x = draw_inv_x(jax.random.fold_in(arg_keys[9], 71), 0)
    inv_y = draw_inv_y(jax.random.fold_in(arg_keys[9], 71), 0)
    spike_x = draw_spike_x(jax.random.fold_in(arg_keys[9], 71), 0)
    spike_y = draw_spike_y(jax.random.fold_in(arg_keys[9], 71), 0)
    marker_force = noise(arg_keys[5], (3, MARKERS), 1.0, 6.0, ((1, 32),))
    marker_kernel = jnp.clip(1.0 * jax.random.uniform(arg_keys[6], (MARKERS, CY), jnp.float32) ** shard_levels(arg_keys[6], (MARKERS, CY), ((0, 32),), -0.2, 0.2), 0.0, 1.0).astype(jnp.bfloat16)
    marker_owner_keys = jax.random.split(jax.random.fold_in(arg_keys[7], 1), MARKERS // M_DEV)
    marker_owner_turns = jax.random.permutation(jax.random.fold_in(arg_keys[7], 3), MARKERS // M_DEV)
    marker_owner = jax.vmap(lambda own, number: deal_out(jax.random.fold_in(arg_keys[7], 2), own, number, M_DEV, N_GX, 1, CAP, 2))(marker_owner_keys, marker_owner_turns).reshape((MARKERS, 1))
    marker_row = plant(jax.random.randint(arg_keys[8], (MARKERS,), 0, NZ * CX), jax.random.fold_in(arg_keys[8], 1), 0, (NZ * CX) - 1).astype(jnp.int32)
    return {"velocity": velocity, "inv_x": inv_x, "inv_y": inv_y, "spike_x": spike_x, "spike_y": spike_y, "marker_force": marker_force, "marker_kernel": marker_kernel, "marker_owner": marker_owner, "marker_row": marker_row}


HIGH = lax.Precision.HIGHEST


def stencil(padded, axis):
    size = padded.shape[axis] - 4
    def cut(start):
        return lax.slice_in_dim(padded, start, start + size, axis=axis)
    return (7.0 / 9.0) * (cut(3) - cut(1)) + (1.0 / 36.0) * (cut(4) - cut(0))


def chain(maps, parts):
    def step(state, item):
        pmap, part = item
        new_state = jnp.einsum('ab,czbl->czal', pmap, state, precision=HIGH) + part
        return new_state, state
    start = jnp.zeros(parts.shape[1:], jnp.float32)
    final, before = lax.scan(step, start, (maps, parts))
    return before


def reference(velocity, inv_x, inv_y, spike_x, spike_y, marker_force, marker_kernel, marker_owner, marker_row):
    padded = jnp.pad(velocity, ((0, 0), (0, 0), (2, 2), (2, 2)))
    rx = stencil(padded[:, :, :, 2:-2], 2)
    ry = stencil(padded[:, :, 2:-2, :], 3)

    blocks_x = inv_x.reshape(N_GX, CX, CX)
    cols_x = spike_x.reshape(N_GX, CX, 2)
    vx = jnp.einsum('dij,czdjy->czdiy', blocks_x, rx.reshape(3, NZ, N_GX, CX, NY), precision=HIGH)
    qx = jnp.moveaxis(vx[:, :, :, CX - 2:, :], 2, 0)
    sx = chain(cols_x[:, CX - 2:, :], qx)
    dx = (vx + jnp.einsum('dia,dczay->czdiy', cols_x, sx, precision=HIGH)).reshape(3, NZ, NX, NY)

    blocks_y = inv_y.reshape(N_GY, CY, CY)
    cols_y = spike_y.reshape(N_GY, CY, 2)
    vy = jnp.einsum('dij,czxdj->czxdi', blocks_y, ry.reshape(3, NZ, NX, N_GY, CY), precision=HIGH)
    qy = jnp.transpose(vy[..., CY - 2:], (3, 0, 1, 4, 2))
    sy = chain(cols_y[:, CY - 2:, :], qy)
    dy = (vy + jnp.einsum('dia,dczax->czxdi', cols_y, sy, precision=HIGH)).reshape(3, NZ, NX, NY)

    owner_all = marker_owner[:, 0].reshape(N_GX, N_GY, M_DEV)
    row_all = marker_row.reshape(N_GX, N_GY, M_DEV)
    force_all = marker_force.reshape(3, N_GX, N_GY, M_DEV)
    kernel_all = marker_kernel.reshape(N_GX, N_GY, M_DEV, CY)
    columns = []
    for column in range(N_GY):
        owner = owner_all[:, column].reshape(-1).astype(jnp.int32)
        row = row_all[:, column].reshape(-1).astype(jnp.int32)
        force_col = force_all[:, :, column].reshape(3, -1)
        kernel_col = kernel_all[:, column].reshape(-1, CY)
        tiles = (force_col.T[:, :, None].astype(jnp.float32) * kernel_col[:, None, :].astype(jnp.float32)).astype(jnp.bfloat16)
        tiles = lax.optimization_barrier(tiles).astype(jnp.float32)
        index = (row // CX) * NX + owner * CX + row % CX
        summed = jnp.zeros((NZ * NX, 3, CY), jnp.float32).at[index].add(tiles)
        columns.append(jnp.transpose(summed, (1, 0, 2)))
    force = jnp.concatenate(columns, axis=2).reshape(3, NZ, NX, NY)

    return velocity + 0.5 * (force - velocity[0:1] * dx - velocity[1:2] * dy)
```

```python
import functools

import jax
import jax.numpy as jnp
from jax import lax
from jax.experimental import pallas as pl
from jax.experimental.pallas import tpu as pltpu
from jax.sharding import PartitionSpec as P

F32, BF16 = jnp.float32, jnp.bfloat16
NEAR, FAR = 7.0 / 9.0, 1.0 / 36.0
COEFS = 16
NT = (((1,), (1,)), ((), ()))
VMEM = pl.BlockSpec(memory_space=pltpu.VMEM)


def params(mib=48):
    return pltpu.CompilerParams(vmem_limit_bytes=mib << 20)


def call(kernel, out_shape, args, scratch=(), flops=0, extra=0, **kw):
    moved = sum(a.size * a.dtype.itemsize for a in jax.tree.leaves((args, out_shape)))
    cost = pl.CostEstimate(flops=flops, bytes_accessed=moved + extra, transcendentals=0)
    return pl.pallas_call(
        kernel, out_shape=out_shape, scratch_shapes=scratch, compiler_params=params(),
        cost_estimate=cost, **kw,
    )(*args)


def split(x):
    hi = x.astype(BF16)
    return hi, (x - hi.astype(F32)).astype(BF16)


def iota(shape, dim):
    return lax.broadcasted_iota(jnp.int32, shape, dim)


def pack_kernel(ker, force, owner, row, *refs, groups, cap, half, width_x, rows, batch):
    outs, (hot, pay, lhs) = refs[:groups], refs[groups:]
    slots, width = ker.shape
    me = lax.axis_index("gx")
    own = owner[...]
    hits = (iota((groups, slots), 0) == own).astype(F32)
    block = min(256, slots)
    tri = (iota((block, block), 0) <= iota((block, block), 1)).astype(BF16)
    carry = jnp.zeros((groups, 1), F32)
    ranks = []
    for b in range(slots // block):
        part = hits[:, b * block : (b + 1) * block]
        count = jnp.dot(part.astype(BF16), tri, preferred_element_type=F32)
        ranks.append(jnp.sum(part * (count + (carry - 1.0)), axis=0, keepdims=True))
        carry = carry + count[:, block - 1 : block]
    rank = jnp.concatenate(ranks, axis=1).astype(jnp.int32)
    place, part = lax.rem(rank, half), lax.div(rank, half)
    hot[...] = (iota((half, slots), 0) == place).astype(F32).astype(BF16)
    pay[:width, :] = ker[...].T
    line = row[...]
    tail = jnp.concatenate(
        [
            force[...].astype(F32),
            lax.div(line, width_x).astype(F32),
            lax.rem(line, width_x).astype(F32),
            jnp.zeros((rows - width - 5, slots), F32),
        ],
        axis=0,
    )
    pay[width:, :] = tail.astype(BF16)
    jobs = [(k, h) for k in range(groups) for h in range(cap // half)]
    for first in range(0, len(jobs), batch):
        some = jobs[first : first + batch]
        for i, (k, h) in enumerate(some):
            dest = lax.rem(me + k, groups)
            keep = jnp.where((own == dest) & (part == h), 1.0, 0.0).astype(BF16)
            lhs[i * rows : (i + 1) * rows, :] = pay[...] * keep
        got = lax.dot_general(
            lhs[: len(some) * rows, :], hot[...], NT, preferred_element_type=F32
        ).astype(BF16)
        for i, (k, h) in enumerate(some):
            outs[k][:, h * half : (h + 1) * half] = got[i * rows : (i + 1) * rows, :]


def pack(ker, force, owner, row, groups, width_x):
    slots, width = ker.shape
    cap = 2 * slots // groups
    half = min(256, cap)
    rows = -(-(width + 5) // 8) * 8
    batch = 4
    out = [jax.ShapeDtypeStruct((rows, cap), BF16)] * groups
    kernel = functools.partial(
        pack_kernel, groups=groups, cap=cap, half=half, width_x=width_x, rows=rows, batch=batch
    )
    return call(
        kernel, out, (ker, force, owner, row),
        scratch=[
            pltpu.VMEM((half, slots), BF16),
            pltpu.VMEM((rows, slots), BF16),
            pltpu.VMEM((batch * rows, slots), BF16),
        ],
        flops=2 * rows * cap * groups * slots,
    )


def spread_kernel(*refs, count, cap, width, width_x, zb, last):
    msgs, refs = refs[:count], refs[count:]
    adds, refs = refs[: 2 if last else 1], refs[2 if last else 1 :]
    out, tile, xhot, zrow, lhs = refs
    step = pl.program_id(0)

    @pl.when(step == 0)
    def _():
        for i, msg in enumerate(msgs):
            cols = slice(i * cap, (i + 1) * cap)
            kern = msg[:width, :]
            tail = msg[width:, :].astype(F32)
            for c in range(3):
                tile[c * width : (c + 1) * width, cols] = (
                    kern.astype(F32) * tail[c : c + 1]
                ).astype(BF16)
            zrow[:, cols] = tail[3:4]
            xs = tail[4:5].astype(jnp.int32)
            xhot[:, cols] = (iota((width_x, cap), 0) == xs).astype(F32).astype(BF16)

    for i in range(zb):
        z = (step * zb + i).astype(F32)
        keep = jnp.where(zrow[...] == z, 1.0, 0.0).astype(BF16)
        lhs[i * width_x : (i + 1) * width_x, :] = xhot[...] * keep
    got = lax.dot_general(lhs[...], tile[...], NT, preferred_element_type=F32)
    for i in range(zb):
        for c in range(3):
            val = got[i * width_x : (i + 1) * width_x, c * width : (c + 1) * width]
            if adds:
                val = val + adds[0][c, i]
            if last:
                val = adds[1][c, i] + 0.5 * val
            out[c, i] = val


def spread(msgs, acc, base, shape):
    comps, depth, width_x, width = shape
    cap = msgs[0].shape[1]
    count = len(msgs)
    zb = 4
    last = base is not None
    adds = [a for a in (acc, base) if a is not None]
    whole = pl.BlockSpec(msgs[0].shape, lambda s: (0, 0))
    block = pl.BlockSpec((comps, zb, width_x, width), lambda s: (0, s, 0, 0))

    def kernel(*refs):
        if acc is None:
            refs_in = refs[:count]
            return spread_first(refs_in, refs[count:])
        spread_kernel(
            *refs, count=count, cap=cap, width=width, width_x=width_x, zb=zb, last=last
        )

    def spread_first(refs_in, rest):
        out, tile, xhot, zrow, lhs = rest
        zero = Zero()
        spread_kernel(
            *refs_in, zero, out, tile, xhot, zrow, lhs,
            count=count, cap=cap, width=width, width_x=width_x, zb=zb, last=False,
        )

    return call(
        kernel, jax.ShapeDtypeStruct(shape, F32), (*msgs, *adds),
        grid=(depth // zb,),
        in_specs=[whole] * count + [block] * len(adds),
        out_specs=block,
        scratch=[
            pltpu.VMEM((comps * width, count * cap), BF16),
            pltpu.VMEM((width_x, count * cap), BF16),
            pltpu.VMEM((1, count * cap), F32),
            pltpu.VMEM((zb * width_x, count * cap), BF16),
        ],
        flops=2 * comps * width * count * cap * depth * width_x,
    )


class Zero:
    def __getitem__(self, key):
        return 0.0


def shifted(g, by):
    size = g.shape[1]
    lane = iota(g.shape, 1)
    moved = pltpu.roll(g, by % size, 1)
    return jnp.where((lane >= by) & (lane < size + by), moved, 0.0)


def stencil_cols(g):
    return NEAR * (shifted(g, 1) - shifted(g, -1)) + FAR * (shifted(g, 2) - shifted(g, -2))


def halo_cols(g):
    n = g.shape[1]
    return (
        -FAR * g[:, 0:1],
        -NEAR * g[:, 0:1] - FAR * g[:, 1:2],
        NEAR * g[:, n - 1 : n] + FAR * g[:, n - 2 : n - 1],
        FAR * g[:, n - 1 : n],
    )


def column(row, size):
    return jnp.broadcast_to(row, (size, row.shape[1])).T


def edge_kernel(vel, inv_x, inv_y, sp_x, sp_y, ex, ey, lr):
    lines, wx, wy = vel.shape
    odd = lax.rem(lax.axis_index("gx"), 2) == 1
    cols = []
    for inv, sp, out, n, other in ((inv_x, sp_x, ex, wx, wy), (inv_y, sp_y, ey, wy, wx)):
        tail = inv[n - 8 :, :]
        local = stencil_cols(tail)
        cols.append([column(local[6 + a : 7 + a], other) for a in range(2)])
        halo = halo_cols(tail)
        rows = [sp[b : b + 1, n - 2 + a : n - 1 + a] for a in range(2) for b in range(2)]
        rows += [halo[b][6 + a : 7 + a] for a in range(2) for b in range(2)]
        rows += [halo[2 + b][6 + a : 7 + a] for a in range(2) for b in range(2)]
        for i, val in enumerate(rows):
            out[6 * lines + i : 6 * lines + i + 1, :] = jnp.broadcast_to(val, (1, other))
        out[6 * lines + len(rows) :, :] = jnp.zeros((COEFS - len(rows), other), F32)

    def one(i, _):
        f = vel[i]
        for data, out, n, cs in ((f, ex, wx, cols[0]), (f.T, ey, wy, cols[1])):
            for a in range(2):
                out[pl.ds(a * lines + i, 1), :] = jnp.sum(cs[a] * data, axis=0, keepdims=True)
                out[pl.ds((2 + a) * lines + i, 1), :] = data[n - 2 + a : n - 1 + a]
                out[pl.ds((4 + a) * lines + i, 1), :] = data[a : a + 1]
        return 0

    lax.fori_loop(0, lines, one, 0, unroll=2)
    lr[...] = jnp.where(odd, ex[2 * lines : 4 * lines, :], ex[4 * lines : 6 * lines, :])


def edges(vel, inv_x, inv_y, sp_x, sp_y):
    lines, wx, wy = vel.shape
    out = (
        jax.ShapeDtypeStruct((6 * lines + COEFS, wy), F32),
        jax.ShapeDtypeStruct((6 * lines + COEFS, wx), F32),
        jax.ShapeDtypeStruct((2 * lines, wy), F32),
    )
    return call(edge_kernel, out, (vel, inv_x, inv_y, sp_x, sp_y), in_specs=[VMEM] * 5, out_specs=(VMEM,) * 3)


def unpack(ref, lines):
    data = [ref[i * lines : (i + 1) * lines, :] for i in range(6)]
    coef = [ref[6 * lines + i : 6 * lines + i + 1, :] for i in range(12)]
    return data[0:2], data[2:4], data[4:6], coef[0:4], coef[4:8], coef[8:12]


def mul(mat, vec):
    return [mat[0] * vec[0] + mat[1] * vec[1], mat[2] * vec[0] + mat[3] * vec[1]]


def matmul2(a, b):
    return [
        a[0] * b[0] + a[1] * b[2], a[0] * b[1] + a[1] * b[3],
        a[2] * b[0] + a[3] * b[2], a[2] * b[1] + a[3] * b[3],
    ]


def add(*vecs):
    return [functools.reduce(lambda p, q: p + q, parts) for parts in zip(*vecs)]


def pick(cond, a, b):
    return [jnp.where(cond, p, q) for p, q in zip(a, b)]


def pair_parts(mine, mate, near, far, lines):
    odd = lax.rem(lax.axis_index("gx"), 2) == 1
    a, b = unpack(mine, lines), unpack(mate, lines)
    even_part = [pick(odd, q, p) for p, q in zip(a, b)]
    odd_part = [pick(odd, p, q) for p, q in zip(a, b)]
    got_near = [near[:lines, :], near[lines:, :]]
    got_far = [far[:lines, :], far[lines:, :]]
    before, after = pick(odd, got_far, got_near), pick(odd, got_near, got_far)
    q0, l0, r0, p0, lo0, hi0 = even_part
    q1, l1, r1, p1, lo1, hi1 = odd_part
    full0 = add(q0, mul(lo0, before), mul(hi0, r1))
    full1 = add(q1, mul(lo1, l0), mul(hi1, after))
    return odd, full0, full1, p0, p1, pick(odd, l0, before), pick(odd, after, r1)


def pair_kernel(mine, mate, near, far, out):
    lines = near.shape[0] // 2
    _, full0, full1, p0, p1, _, _ = pair_parts(mine, mate, near, far, lines)
    total, joined = add(mul(p1, full0), full1), matmul2(p1, p0)
    for a in range(2):
        out[a * lines : (a + 1) * lines, :] = total[a]
    for i in range(4):
        out[2 * lines + i : 2 * lines + i + 1, :] = joined[i]
    out[2 * lines + 4 :, :] = jnp.zeros((4, out.shape[1]), F32)


def base_kernel(*refs, pairs, ring, depth):
    vel, inv_x, inv_y, sp_x, sp_y, mine, mate, near, far, mine_y = refs[:10]
    before, around = refs[10 : 10 + pairs], refs[10 + pairs : 10 + pairs + ring]
    out, wgt_x, wgt_y, ext_x, ext_y = refs[10 + pairs + ring :]
    comps, _, wx, wy = vel.shape
    lines = comps * depth
    step = pl.program_id(0)

    @pl.when(step == 0)
    def _():
        ext_x[...] = jnp.zeros(ext_x.shape, F32)
        ext_y[...] = jnp.zeros(ext_y.shape, F32)
        for inv, sp, wgt in ((inv_x, sp_x, wgt_x), (inv_y, sp_y, wgt_y)):
            g = inv[...]
            n = g.shape[0]
            hi, lo = split(stencil_cols(g))
            wgt[:, 0 * n : 1 * n] = hi
            wgt[:, 1 * n : 2 * n] = lo
            wgt[:, 2 * n : 3 * n] = hi
            lane = iota((n, n), 1)
            extra = jnp.zeros((n, n), F32)
            cols = list(halo_cols(g)) + [column(sp[b : b + 1, :], n) for b in range(2)]
            for i, col in enumerate(cols):
                extra = jnp.where(lax.rem(lane, 16) == i, col, extra)
            hi, lo = split(extra)
            mixed = jnp.where((lane >= 16) & (lane < 32), lo.astype(F32), hi.astype(F32))
            wgt[:, 3 * n : 4 * n] = jnp.where(lane < 48, mixed, 0.0).astype(BF16)

        odd, full0, _, p0, _, low, high = pair_parts(mine, mate, near, far, lines)
        state = None
        for h in reversed(range(pairs)):
            total = [before[h][a * lines : (a + 1) * lines, :] for a in range(2)]
            mat = [before[h][2 * lines + i : 2 * lines + i + 1, :] for i in range(4)]
            state = total if state is None else add(mul(mat, state), total)
        if state is None:
            state = [jnp.zeros_like(low[0])] * 2
        state = pick(odd, add(mul(p0, state), full0), state)
        for i, val in enumerate(low + high + state):
            for rep in range(3):
                ext_x[:, 16 * rep + i, :] = val

        me = lax.axis_index("gy")
        got = [unpack(mine_y, lines)] + [unpack(ref, lines) for ref in around]
        none = [jnp.zeros_like(low[0])] * 2
        state = none
        for k in range(ring, 0, -1):
            q, _, _, p, lo, hi = got[k]
            left = pick(me >= k + 1, got[k + 1][1], none) if k < ring else none
            right = got[k - 1][2]
            new = add(mul(p, state), q, mul(lo, left), mul(hi, right))
            state = pick(me >= k, new, none)
        low = pick(me >= 1, got[1][1], none) if ring else none
        high = pick(me + 1 <= ring, got[ring][2], none) if ring else none
        for i, val in enumerate(low + high + state):
            for rep in range(3):
                ext_y[:, 16 * rep + i, :] = val

    f = [vel[c, 0] for c in range(comps)]
    hi, lo = zip(*[split(x) for x in f])
    pad = jnp.zeros((ext_x.shape[1], wy), F32)
    row = iota((wx, wy), 0)
    lane = iota((wx, wy), 1)

    def rows_of(ext, c):
        part = ext[c * depth + step]
        return jnp.concatenate([part, jnp.zeros((wx - part.shape[0], wy), F32)], axis=0)

    ext = []
    for c in range(comps):
        e_hi, e_lo = split(rows_of(ext_x, c))
        ext.append(jnp.where(row < 32, e_hi.astype(F32), e_lo.astype(F32)).astype(BF16))
    rhs = jnp.concatenate(
        [jnp.concatenate(part, axis=1) for part in (hi, hi, lo, ext)], axis=0
    )
    dx = jnp.dot(wgt_x[...], rhs, preferred_element_type=F32)
    ext = []
    for c in range(comps):
        e_hi, e_lo = split(rows_of(ext_y, c).T)
        ext.append(jnp.where(lane < 32, e_hi.astype(F32), e_lo.astype(F32)).astype(BF16))
    lhs = jnp.concatenate(
        [jnp.concatenate(part, axis=0) for part in (hi, hi, lo, ext)], axis=1
    )
    dy = lax.dot_general(lhs, wgt_y[...], NT, preferred_element_type=F32)
    for c in range(comps):
        moved = f[0] * dx[:, c * wy : (c + 1) * wy] + f[1] * dy[c * wx : (c + 1) * wx]
        out[c, 0] = f[c] - 0.5 * moved


def base_step(vel, small, msgs_x, own_y, before, around):
    comps, depth, wx, wy = vel.shape
    pairs, ring = len(before), len(around)
    block = pl.BlockSpec((comps, 1, wx, wy), lambda s: (0, s, 0, 0))
    rest = (*small, *msgs_x, own_y, *before, *around)
    kernel = functools.partial(base_kernel, pairs=pairs, ring=ring, depth=depth)
    return call(
        kernel, jax.ShapeDtypeStruct(vel.shape, F32), (vel, *rest),
        grid=(depth,),
        in_specs=[block] + [pl.BlockSpec(a.shape, lambda s: (0, 0)) for a in rest],
        out_specs=block,
        scratch=[
            pltpu.VMEM((wx, 4 * wx), BF16),
            pltpu.VMEM((wy, 4 * wy), BF16),
            pltpu.VMEM((comps * depth, 48, wy), F32),
            pltpu.VMEM((comps * depth, 48, wx), F32),
        ],
        flops=2 * 8 * wx * wx * wy * comps * depth,
    )


def local(
    velocity, inv_x, inv_y, spike_x, spike_y, marker_force, marker_kernel, marker_owner, marker_row
):
    shape = velocity.shape
    comps, depth, width_x, width_y = shape
    gx, gy = lax.axis_size("gx"), lax.axis_size("gy")
    slots = marker_row.shape[0]

    packed = pack(
        marker_kernel, marker_force, marker_owner.reshape(1, slots),
        marker_row.reshape(1, slots), gx, width_x,
    )
    order = list(range(gx - 1, 0, -1))
    got = {}
    for k in order:
        got[k] = lax.ppermute(packed[k], "gx", [(i, (i + k) % gx) for i in range(gx)])

    flat = velocity.reshape(comps * depth, width_x, width_y)
    small = (inv_x, inv_y, spike_x.T, spike_y.T)
    ex, ey, lr = edges(flat, *small)
    mate = lax.ppermute(ex, "gx", [(i, i ^ 1) for i in range(gx)])
    near, far = (
        lax.ppermute(
            lr, "gx",
            [(i, i + by if i % 2 else i - by) for i in range(gx)
             if 0 <= (i + by if i % 2 else i - by) < gx],
        )
        for by in (1, 2)
    )
    around = [
        lax.ppermute(ey, "gy", [(i, (i + k) % gy) for i in range(gy)]) for k in range(1, gy)
    ]
    lines = comps * depth
    pair = call(
        pair_kernel, jax.ShapeDtypeStruct((2 * lines + 8, width_y), F32), (ex, mate, near, far),
        in_specs=[VMEM] * 4, out_specs=VMEM,
    )
    before = [
        lax.ppermute(pair, "gx", [(i, i + 2 * h) for i in range(gx - 2 * h)])
        for h in range(1, gx // 2)
    ]
    base = base_step(velocity, small, (ex, mate, near, far), ey, before, around)

    acc = spread([packed[0]] + [got[k] for k in order[:2]], None, None, shape)
    acc = spread([got[k] for k in order[2:-2]], acc, None, shape)
    return spread([got[k] for k in order[-2:]], acc, base, shape)


def solution(mesh):
    return jax.shard_map(
        local,
        mesh=mesh,
        in_specs=(
            P(None, None, "gx", "gy"),
            P("gx", None),
            P("gy", None),
            P("gx", None),
            P("gy", None),
            P(None, ("gx", "gy")),
            P(("gx", "gy"), None),
            P(("gx", "gy"), None),
            P(("gx", "gy")),
        ),
        out_specs=P(None, None, "gx", "gy"),
        check_vma=False,
    )
```
